256 devices in a mesh: seq: 64 (over z_hi, x, y), mp: 4 (over z_lo, core).
Axes of the slice: x: 4, y: 4, z: 8 (z_hi: 4, z_lo: 2; z = z_hi * 2 + z_lo), core: 2. Of those that a mesh axis runs over, the one named last changes fastest.
Arguments:
- byte_values: int32 [65536], P('seq'), may hold values from 0 to 255
- hash_owner: int32 [65536, 1], P('seq'), may hold values from 0 to 63; in each aligned block of 1024 rows (0 to 1023, 1024 to 2047, ...) at most 32 rows name the same one
- hash_slot: int32 [65536], P('seq'), may hold values from 0 to 4095
- patch_start: int32 [2048], P('seq'), may hold values from 0 to 65535, as said below
- byte_table: bfloat16 [256, 1280], P(None, 'mp'), may hold values from -6 to 6
- hash_table: bfloat16 [262144, 1280], P('seq', 'mp'), may hold values from -6 to 6
- norm_gains: float32 [3, 1280], replicated, may hold values from 0.5 to 1.5
- w_query: bfloat16 [1280, 1280], P(None, 'mp'), may hold values from -8 to 8
- w_key: bfloat16 [1280, 1280], P(None, 'mp'), may hold values from -8 to 8
- w_value: bfloat16 [1280, 1280], P(None, 'mp'), may hold values from -0.15625 to 0.15625
- w_attn_out: bfloat16 [1280, 1280], P('mp'), may hold values from -0.15625 to 0.15625
- w_gate: bfloat16 [1280, 3584], P('seq', 'mp'), may hold values from -0.15625 to 0.15625
- w_up: bfloat16 [1280, 3584], P('seq', 'mp'), may hold values from -0.15625 to 0.15625
- w_down: bfloat16 [3584, 1280], P('mp', 'seq'), may hold values from -0.09375 to 0.09375
- w_cross_query: bfloat16 [1280, 1280], P(None, 'mp'), may hold values from -8 to 8
- w_cross_key: bfloat16 [1280, 1280], P(None, 'mp'), may hold values from -8 to 8
- w_cross_value: bfloat16 [1280, 1280], P(None, 'mp'), may hold values from -0.15625 to 0.15625
- w_cross_out: bfloat16 [1280, 1280], P('mp'), may hold values from -0.15625 to 0.15625
- w_global: bfloat16 [1280, 4096], P(None, 'mp'), may hold values from -0.15625 to 0.15625
Outputs:
- patches: bfloat16 [2048, 4096], P('seq', 'mp')
The draws below stay inside these ranges and needn't reach their ends.
Inputs may be any that keep to these rules, and one draw needn't show every extreme that they name: `hash_owner`: in each aligned block of 1024 rows (the bytes of one range) every value is named by at most 32 bytes; in some blocks one value is named by exactly 32 bytes. patch_start rises strictly and begins with 0. The patches p with p // 32 = s start at or after s * 1024 - 512 and end at or before (s + 1) * 1024 + 512; in every draw some group starts exactly 512 bytes before its range and some group ends exactly 512 bytes after its range.
All inputs are finite; a program needn't handle non-finite values.
Results may differ from the reference program's by a relative error of at most 0.025.
Values may be sent and summed in bfloat16 or wider, within the bound.
No kernel may reach another device: no remote copies, remote signals or barrier semaphores. Data moves between devices by JAX's collectives and lax.ppermute only.
A program may use at most 128 MiB of HBM per device.

```python
import math
import jax
import jax.numpy as jnp
import numpy as np
from jax import lax

D = 1280
HEADS = 20
HD = 64
FF = 3584
GD = 4096
WINDOW = 512
HROW_DEV = 4096
BYTES_DEV = 1024
PATCH_DEV = 32
REACH = 512
BYTES = 65536
NPATCH = 2048
HASH_ROWS = 262144
CAP = 32
N_SEQ = 64
N_MP = 4


def query_key_pair(key, salt):
    base = jax.random.fold_in(key, salt)
    first_key, second_key = jax.random.split(base, 2)
    key_weight = jax.random.normal(first_key, (D, D), jnp.float32) * D ** (-0.5)
    noise = jax.random.normal(second_key, (D, D), jnp.float32) * D ** (-0.5)
    query_weight = noise
    return (query_weight, key_weight)


def draw_w_query(key, part):
    return query_key_pair(key, 11)[0].astype(jnp.bfloat16)


def draw_w_key(key, part):
    return query_key_pair(key, 11)[1].astype(jnp.bfloat16)


def draw_w_cross_query(key, part):
    return query_key_pair(key, 23)[0].astype(jnp.bfloat16)


def draw_w_cross_key(key, part):
    return query_key_pair(key, 23)[1].astype(jnp.bfloat16)


def draw_patch_start(key, part):
    owners = BYTES // BYTES_DEV
    base = jax.random.fold_in(key, 29)
    first_key, second_key, third_key, fourth_key = jax.random.split(base, 4)
    raw = jax.random.randint(first_key, (owners,), -(REACH - PATCH_DEV), REACH - PATCH_DEV + 1)
    low_at = jax.random.randint(second_key, (), 0, owners - 1)
    offset = jax.random.randint(third_key, (), 0, owners - 3)
    high_at = (low_at + 1 + offset) % (owners - 1)
    index = jnp.arange(owners, dtype=jnp.int32)
    drift = jnp.where(index == low_at, -REACH, raw)
    drift = jnp.where(index == high_at, REACH, drift)
    drift = jnp.where(index == owners - 1, 0, drift)
    previous = jnp.concatenate([jnp.zeros((1,), jnp.int32), drift[:-1]])
    totals = BYTES_DEV + drift - previous
    weights = jax.random.randint(fourth_key, (owners, PATCH_DEV), 1, 17)
    running = jnp.cumsum(weights, axis=1)
    whole = running[:, -1:]
    spare = (totals - PATCH_DEV)[:, None]
    cuts = spare * running // whole
    earlier_cuts = jnp.concatenate([jnp.zeros((owners, 1), jnp.int32), cuts[:, :-1]], axis=1)
    lengths = 1 + cuts - earlier_cuts
    inner = jnp.cumsum(lengths, axis=1) - lengths
    owner_start = index * BYTES_DEV + previous
    return (owner_start[:, None] + inner).reshape(-1).astype(jnp.int32)


def plant(entries, stream_key, low, high):
    longest = entries.shape.index(max(entries.shape))
    spots = []
    for shift in (0, 1):
        where = [jax.random.randint(jax.random.fold_in(stream_key, axis), (), 0, length) for axis, length in enumerate(entries.shape)]
        where[longest] = (where[longest] + shift) % entries.shape[longest]
        spots.append(tuple(where))
    return entries.at[spots[0]].set(low).at[spots[1]].set(high)


def level_of(key, extent, pieces, least, top_value):
    factor_of, own = 1.0, jax.random.fold_in(key, 6)
    for position, blocks in pieces:
        steps = jnp.exp(jax.random.uniform(jax.random.fold_in(own, position), (blocks,), jnp.float32, least / len(pieces), top_value / len(pieces)))
        factor_of = factor_of * jnp.repeat(steps, extent[position] // blocks).reshape([-1 if axis == position else 1 for axis in range(len(extent))])
    return factor_of


def rank_table(number_of, skew):
    loads = [(1 << 20) // math.isqrt(rank ** skew) + 1 for rank in range(1, number_of + 1)]
    scale = 1 + sum(loads) // (1 << 30)
    return np.cumsum(np.array([max(1, weight // scale) for weight in loads]))


def ranked(stream_key, dims, number_of, slope):
    table = rank_table(number_of, slope)
    ticket = jax.random.randint(jax.random.fold_in(stream_key, 1), dims, 0, int(table[number_of - 1]))
    grade = jnp.searchsorted(jnp.asarray(table, jnp.int32), ticket, side="right")
    return jax.random.permutation(jax.random.fold_in(stream_key, 2), number_of)[grade].astype(jnp.int32)


def routed_block(stream_key, own, number, rows, count, top, most, slope):
    order = jax.random.permutation(stream_key, count)
    crowded, usual = portions_of(count, rows * top, most, slope, True), portions_of(count, rows * top, most, slope, False)
    places = jnp.arange(count)

    def named(sizes, turn):
        used = int((sizes > 0).sum())
        fixed = max(1, used // 4)
        moved = fixed + (places - fixed + turn * (used - fixed)) % max(1, count - fixed)
        return jnp.zeros((count,), jnp.int32).at[order[jnp.where(places < fixed, places, moved)]].set(jnp.asarray(sizes, jnp.int32))

    sizes = jnp.where(number % 4 == 0, named(crowded, number // 4), named(usual, number - number // 4 - 1))
    mixed = jax.random.permutation(jax.random.fold_in(own, 3), count)
    donor, sink = mixed[0:count // 2 * 2:2], mixed[1:count // 2 * 2:2]
    margin = jnp.minimum(sizes[donor] - 1, most - sizes[sink]) // 2
    margin = jnp.where((donor == order[0]) | (sink == order[0]) | (sizes[sink] == 0), 0, jnp.maximum(margin, 0))
    moved = jax.random.randint(jax.random.fold_in(own, 4), (count // 2,), 0, 1 << 20) % (margin + 1)
    sizes = sizes.at[donor].add(-moved).at[sink].add(moved)
    items = jnp.searchsorted(jnp.cumsum(sizes), jnp.arange(rows * top), side="right").astype(jnp.int32)
    listing = items.reshape(top, rows).T
    listing = listing[jax.random.permutation(jax.random.fold_in(own, 1), rows)]
    turn = jax.random.randint(jax.random.fold_in(own, 2), (rows, 1), 0, top)
    return jnp.take_along_axis(listing, (jnp.arange(top)[None, :] + turn) % top, axis=1)


def portions_of(number_of, total, limit, skew, full):
    weights = [(1 << 20) // math.isqrt(rank ** skew) + 1 for rank in range(1, number_of + 1)]
    largest = limit if full else min(limit, max(-(-total // number_of), total * weights[0] // sum(weights)))
    least = 1 if total - largest >= number_of - 1 else 0
    given, rest = [largest] + [least] * (number_of - 1), total - largest - least * (number_of - 1)
    while rest > 0:
        free = [i for i in range(1, number_of) if given[i] < largest] or [i for i in range(1, number_of) if given[i] < limit]
        whole, left = sum([weights[i] for i in free]), rest
        for i in free:
            extra = min(limit - given[i], max(1, left * weights[i] // whole), rest)
            given[i] = given[i] + extra
            rest = rest - extra
    return np.array(given)


def normal_values(key, shape, spread, limit, pieces=(), held_as=jnp.bfloat16):
    result = jax.random.normal(key, shape, jnp.float32) * spread
    if len(pieces) > 0:
        result = level_of(key, shape, pieces, -0.22, 0.18) * result
    return jnp.clip(result, min=-limit, max=limit).astype(held_as)


def setup_inputs(seed: int = 0) -> dict:
    streams_of = jax.random.split(jax.random.key(seed), 20)
    byte_values = plant(ranked(streams_of[0], (BYTES,), 256, 2), jax.random.fold_in(streams_of[0], 3), 0, 255).astype(jnp.int32)
    hash_owner_keys = jax.random.split(jax.random.fold_in(streams_of[1], 1), BYTES // BYTES_DEV)
    hash_owner_turns = jax.random.permutation(jax.random.fold_in(streams_of[1], 3), BYTES // BYTES_DEV)
    hash_owner = jax.vmap(lambda own, number: routed_block(jax.random.fold_in(streams_of[1], 2), own, number, BYTES_DEV, BYTES // BYTES_DEV, 1, CAP, 2))(hash_owner_keys, hash_owner_turns).reshape((BYTES, 1))
    hash_slot = plant(jax.random.randint(streams_of[2], (BYTES,), 0, HROW_DEV), jax.random.fold_in(streams_of[2], 1), 0, HROW_DEV - 1).astype(jnp.int32)
    patch_start = draw_patch_start(jax.random.fold_in(streams_of[19], 71), 0)
    byte_table = normal_values(streams_of[4], (256, D), 1.0, 6.0, ((1, 4),))
    hash_table = normal_values(streams_of[5], (HASH_ROWS, D), 1.0, 6.0, ((0, 64), (1, 4)))
    norm_gains = jnp.clip(1.0 + 0.1 * jax.random.normal(streams_of[6], (3, D), jnp.float32), 0.5, 1.5)
    w_query = draw_w_query(jax.random.fold_in(streams_of[19], 71), 0)
    w_key = draw_w_key(jax.random.fold_in(streams_of[19], 71), 0)
    w_value = normal_values(streams_of[9], (D, D), D ** -0.5, 0.15625, ((1, 4),))
    w_attn_out = normal_values(streams_of[10], (D, D), D ** -0.5, 0.15625, ((0, 4),))
    w_gate = normal_values(streams_of[11], (D, FF), D ** -0.5, 0.15625, ((0, 64), (1, 4)))
    w_up = normal_values(streams_of[12], (D, FF), D ** -0.5, 0.15625, ((0, 64), (1, 4)))
    w_down = normal_values(streams_of[13], (FF, D), FF ** -0.5, 0.09375, ((0, 4), (1, 64)))
    w_cross_query = draw_w_cross_query(jax.random.fold_in(streams_of[19], 71), 0)
    w_cross_key = draw_w_cross_key(jax.random.fold_in(streams_of[19], 71), 0)
    w_cross_value = normal_values(streams_of[16], (D, D), D ** -0.5, 0.15625, ((1, 4),))
    w_cross_out = normal_values(streams_of[17], (D, D), D ** -0.5, 0.15625, ((0, 4),))
    w_global = normal_values(streams_of[18], (D, GD), D ** -0.5, 0.15625, ((1, 4),))
    return dict(byte_values=byte_values, hash_owner=hash_owner, hash_slot=hash_slot, patch_start=patch_start, byte_table=byte_table, hash_table=hash_table, norm_gains=norm_gains, w_query=w_query, w_key=w_key, w_value=w_value, w_attn_out=w_attn_out, w_gate=w_gate, w_up=w_up, w_down=w_down, w_cross_query=w_cross_query, w_cross_key=w_cross_key, w_cross_value=w_cross_value, w_cross_out=w_cross_out, w_global=w_global)


def rms_scale(values, gain):
    return values * lax.rsqrt(lax.optimization_barrier(jnp.mean(values * values, axis=-1, keepdims=True)) + 1e-05) * gain

def rounded(values):
    return lax.optimization_barrier(values.astype(jnp.bfloat16)).astype(jnp.float32)

def masked_softmax(scores, valid):
    scores = jnp.where(valid, scores, -1e+30)
    highest = lax.optimization_barrier(jnp.max(scores, axis=-1, keepdims=True))
    raised = jnp.exp(scores - highest)
    return raised / lax.optimization_barrier(jnp.sum(raised, axis=-1, keepdims=True))

def grouped_sum(left, right, groups):
    width = left.shape[1] // groups
    total = jnp.zeros((left.shape[0], right.shape[1]), jnp.float32)
    for group in range(groups):
        term = jnp.dot(left[:, group * width:(group + 1) * width], right[group * width:(group + 1) * width], preferred_element_type=jnp.float32)
        total = total + rounded(term)
    return total

def reference(byte_values, hash_owner, hash_slot, patch_start, byte_table, hash_table, norm_gains, w_query, w_key, w_value, w_attn_out, w_gate, w_up, w_down, w_cross_query, w_cross_key, w_cross_value, w_cross_out, w_global):
    row_ids = (hash_owner[:, 0] * HROW_DEV + hash_slot).astype(jnp.int32)
    hash_rows = jnp.take(hash_table, row_ids, axis=0).astype(jnp.float32)
    byte_rows = jnp.take(byte_table, byte_values, axis=0).astype(jnp.float32)
    embed = (byte_rows + hash_rows).astype(jnp.bfloat16)
    residual = embed.astype(jnp.float32)
    normed = rms_scale(residual, norm_gains[0]).astype(jnp.bfloat16)
    queries = jnp.dot(normed, w_query, preferred_element_type=jnp.float32).astype(jnp.bfloat16)
    keys = jnp.dot(normed, w_key, preferred_element_type=jnp.float32).astype(jnp.bfloat16)
    values = jnp.dot(normed, w_value, preferred_element_type=jnp.float32).astype(jnp.bfloat16)
    padding = jnp.zeros((WINDOW, D), jnp.bfloat16)
    key_span = jnp.concatenate([padding, keys], axis=0)
    value_span = jnp.concatenate([padding, values], axis=0)

    def attend(block):
        start = block * WINDOW
        query_block = lax.dynamic_slice_in_dim(queries, start, WINDOW, 0).astype(jnp.float32).reshape(WINDOW, HEADS, HD)
        key_block = lax.dynamic_slice_in_dim(key_span, start, 2 * WINDOW, 0).astype(jnp.float32).reshape(2 * WINDOW, HEADS, HD)
        value_block = lax.dynamic_slice_in_dim(value_span, start, 2 * WINDOW, 0).astype(jnp.float32).reshape(2 * WINDOW, HEADS, HD)
        query_pos = start + jnp.arange(WINDOW, dtype=jnp.int32)
        key_pos = start - WINDOW + jnp.arange(2 * WINDOW, dtype=jnp.int32)
        valid = (key_pos[None, :] <= query_pos[:, None]) & (key_pos[None, :] > query_pos[:, None] - WINDOW) & (key_pos[None, :] >= 0)
        scores = jnp.einsum('qhd,khd->hqk', query_block, key_block) * HD ** (-0.5)
        weights = rounded(masked_softmax(scores, valid[None]))
        mixed = jnp.einsum('hqk,khd->qhd', weights, value_block)
        return mixed.astype(jnp.bfloat16).reshape(WINDOW, D)
    heads_out = lax.map(attend, jnp.arange(BYTES // WINDOW, dtype=jnp.int32)).reshape(BYTES, D)
    residual = residual + grouped_sum(heads_out, w_attn_out, N_MP)
    normed = rms_scale(residual, norm_gains[1]).astype(jnp.bfloat16)

    def feed_forward(block_rows):
        gate = jnp.dot(block_rows, w_gate, preferred_element_type=jnp.float32)
        lifted = jnp.dot(block_rows, w_up, preferred_element_type=jnp.float32)
        hidden = (jax.nn.silu(gate) * lifted).astype(jnp.bfloat16)
        return grouped_sum(hidden, w_down, N_MP)
    residual = residual + lax.map(feed_forward, normed.reshape(N_SEQ, BYTES_DEV, D)).reshape(BYTES, D)
    encoded = rms_scale(residual, norm_gains[2]).astype(jnp.bfloat16)
    cross_keys = jnp.dot(encoded, w_cross_key, preferred_element_type=jnp.float32).astype(jnp.bfloat16)
    cross_values = jnp.dot(encoded, w_cross_value, preferred_element_type=jnp.float32).astype(jnp.bfloat16)
    framed_states = jnp.pad(encoded, ((REACH, REACH), (0, 0)))
    framed_keys = jnp.pad(cross_keys, ((REACH, REACH), (0, 0)))
    framed_values = jnp.pad(cross_values, ((REACH, REACH), (0, 0)))
    patch_end = jnp.concatenate([patch_start[1:], jnp.full((1,), BYTES, dtype=jnp.int32)])
    frame_len = BYTES_DEV + 2 * REACH

    def pool(owner):
        first = owner * BYTES_DEV
        states = lax.dynamic_slice_in_dim(framed_states, first, frame_len, 0)
        frame_keys = lax.dynamic_slice_in_dim(framed_keys, first, frame_len, 0).astype(jnp.float32).reshape(frame_len, HEADS, HD)
        frame_values = lax.dynamic_slice_in_dim(framed_values, first, frame_len, 0).astype(jnp.float32).reshape(frame_len, HEADS, HD)
        starts = lax.dynamic_slice_in_dim(patch_start, owner * PATCH_DEV, PATCH_DEV, 0)
        stops = lax.dynamic_slice_in_dim(patch_end, owner * PATCH_DEV, PATCH_DEV, 0)
        frame_pos = first - REACH + jnp.arange(frame_len, dtype=jnp.int32)
        member = (frame_pos[None, :] >= starts[:, None]) & (frame_pos[None, :] < stops[:, None])
        counts = lax.optimization_barrier(jnp.sum(member.astype(jnp.float32), axis=1))
        pooled = jnp.dot(member.astype(jnp.bfloat16), states, preferred_element_type=jnp.float32) / counts[:, None]
        pooled_rows = pooled.astype(jnp.bfloat16)
        cross_queries = rounded(jnp.dot(pooled_rows, w_cross_query, preferred_element_type=jnp.float32)).reshape(PATCH_DEV, HEADS, HD)
        scores = jnp.einsum('phd,khd->hpk', cross_queries, frame_keys) * HD ** (-0.5)
        weights = rounded(masked_softmax(scores, member[None]))
        cross_heads = jnp.einsum('hpk,khd->phd', weights, frame_values).astype(jnp.bfloat16).reshape(PATCH_DEV, D)
        mixed = jnp.dot(cross_heads, w_cross_out, preferred_element_type=jnp.float32)
        patch_hidden = (pooled + mixed).astype(jnp.bfloat16)
        return jnp.dot(patch_hidden, w_global, preferred_element_type=jnp.float32).astype(jnp.bfloat16)
    return lax.map(pool, jnp.arange(N_SEQ, dtype=jnp.int32)).reshape(NPATCH, GD)
```

```python
import functools

import jax
import jax.numpy as jnp
from jax import lax
from jax.experimental import pallas as pl
from jax.experimental.pallas import tpu as pltpu
from jax.sharding import PartitionSpec as P

HD = 64
WINDOW = 512
REACH = 512
BLOCK = 256
FAR = 1 << 30
ON_CHIP = [(0, 1), (1, 0), (2, 3), (3, 2)]
ACROSS = [(0, 2), (2, 0), (1, 3), (3, 1)]
DIAGONAL = [(0, 3), (3, 0), (1, 2), (2, 1)]


F32 = jnp.float32
BF16 = jnp.bfloat16


def dot00(a, b):
    return lax.dot_general(a, b, (((0,), (0,)), ((), ())), preferred_element_type=F32)


def chip_shift(value):
    return lax.ppermute(value, "mp", ON_CHIP)


def cross_shift(value):
    return lax.ppermute(value, "mp", ACROSS)


def shifted(value, steps):
    count = lax.axis_size("seq")
    first, last = (max(0, -steps), min(count, count - steps))
    return lax.ppermute(value, "seq", [(i, i + steps) for i in range(first, last)])


def gathered(value):
    across = cross_shift(value)
    beside = chip_shift(value)
    return [value, beside, across, chip_shift(across)]


def attend(start_ref, q_ref, k_ref, v_ref, o_ref):
    length = q_ref.shape[1]
    kk = lax.broadcasted_iota(jnp.int32, (BLOCK, BLOCK), 0)
    qq = lax.broadcasted_iota(jnp.int32, (BLOCK, BLOCK), 1)
    tri_low = kk > qq
    tri_high = kk <= qq
    blocks = WINDOW // BLOCK
    first = start_ref[0]
    for b in range(length // BLOCK):
        q = q_ref[:, b * BLOCK : (b + 1) * BLOCK]
        parts = []
        for t in range(blocks + 1):
            at = b * BLOCK + t * BLOCK
            s = dot00(k_ref[:, at : at + BLOCK], q)
            if t == 0:
                ok = tri_low
            elif t == blocks:
                ok = tri_high
            else:
                ok = None
            if at < WINDOW:
                live = kk + at >= first
                ok = live if ok is None else ok & live
            if ok is not None:
                s = jnp.where(ok, s, -1e30)
            parts.append(s)
        highest = functools.reduce(
            jnp.maximum, [jnp.max(s, axis=0, keepdims=True) for s in parts]
        )
        total = jnp.zeros((1, BLOCK), F32)
        acc = jnp.zeros((HD, BLOCK), F32)
        for t, s in enumerate(parts):
            at = b * BLOCK + t * BLOCK
            p = jnp.exp((s - highest) * (HD**-0.5))
            total = total + jnp.sum(p, axis=0, keepdims=True)
            acc = acc + jnp.dot(
                v_ref[:, at : at + BLOCK], p.astype(BF16), preferred_element_type=F32
            )
        o_ref[:, b * BLOCK : (b + 1) * BLOCK] = (acc / total).astype(BF16)


def attention(start, q, k, v):
    width, length = q.shape
    span = k.shape[1]
    return pl.pallas_call(
        attend,
        grid_spec=pltpu.PrefetchScalarGridSpec(
            num_scalar_prefetch=1,
            grid=(width // HD,),
            in_specs=[
                pl.BlockSpec((HD, length), lambda h, s: (h, 0)),
                pl.BlockSpec((HD, span), lambda h, s: (h, 0)),
                pl.BlockSpec((HD, span), lambda h, s: (h, 0)),
            ],
            out_specs=pl.BlockSpec((HD, length), lambda h, s: (h, 0)),
        ),
        out_shape=jax.ShapeDtypeStruct((width, length), BF16),
        name="attend",
    )(start, q, k, v)


def column_scale(values):
    return lax.rsqrt(jnp.mean(values * values, axis=0, keepdims=True) + 1e-05)


def per_device(
    byte_values,
    hash_owner,
    hash_slot,
    patch_start,
    byte_table,
    hash_table,
    norm_gains,
    w_query,
    w_key,
    w_value,
    w_attn_out,
    w_gate,
    w_up,
    w_down,
    w_cross_query,
    w_cross_key,
    w_cross_value,
    w_cross_out,
    w_global,
):
    seq_count = lax.axis_size("seq")
    position = lax.axis_index("seq")
    group = lax.axis_size("mp")
    me = lax.axis_index("mp")
    core = me % 2
    chip = me // 2
    length = byte_values.shape[0]
    quarter = length // group
    half = length // 2
    width = w_query.shape[1]
    features = w_query.shape[0]
    hidden_width = w_gate.shape[1]
    capacity = 2 * length // seq_count

    packed = jnp.concatenate([w_gate, w_up, w_down.T], axis=1)
    ffn = lax.all_gather(packed, "seq", axis=0, tiled=True)

    before_start = shifted(patch_start, 1)
    after_start = shifted(patch_start, -1)
    after_start = jnp.where(position == seq_count - 1, FAR, after_start)

    owner = hash_owner[:, 0]
    owner_hot = (owner[:, None] == jnp.arange(seq_count, dtype=jnp.int32)[None, :]).astype(BF16)
    line = jnp.arange(length, dtype=jnp.int32)
    earlier = (line[:, None] > line[None, :]).astype(BF16)
    before = jnp.dot(earlier, owner_hot, preferred_element_type=F32)
    order = jnp.sum(before * owner_hot.astype(F32), axis=1).astype(jnp.int32)
    requests = jnp.zeros((seq_count, capacity), jnp.int32).at[owner, order].set(hash_slot)
    wanted = lax.all_to_all(requests, "seq", split_axis=0, concat_axis=0, tiled=True)
    found = jnp.take(hash_table, wanted, axis=0, mode="clip")
    fetched = lax.all_to_all(found, "seq", split_axis=0, concat_axis=0, tiled=True)
    fetched = fetched.reshape(seq_count * capacity, width)
    place = owner * capacity + order
    row_hot = (
        jnp.arange(seq_count * capacity, dtype=jnp.int32)[:, None] == place[None, :]
    ).astype(BF16)
    byte_hot = (jnp.arange(256, dtype=jnp.int32)[:, None] == byte_values[None, :]).astype(BF16)
    embed = (dot00(byte_table, byte_hot) + dot00(fetched, row_hot)).astype(BF16)

    def by_neighbour(value, size):
        return jnp.concatenate(
            [lax.dynamic_slice_in_dim(value, (me ^ k) * size, size, 0) for k in range(group)],
            axis=0,
        )

    w_qkv = by_neighbour(jnp.concatenate([w_query, w_key, w_value], axis=1), width)
    gain_first = by_neighbour(norm_gains[0], width)
    pieces = gathered(embed)
    squares = sum(
        jnp.sum(jnp.square(p.astype(F32)), axis=0, keepdims=True) for p in pieces
    )
    scale = lax.rsqrt(squares / features + 1e-05)
    normed = jnp.concatenate(
        [
            (p.astype(F32) * scale * gain_first[k * width : (k + 1) * width, None]).astype(BF16)
            for k, p in enumerate(pieces)
        ],
        axis=0,
    )
    own = jnp.concatenate(
        [lax.dynamic_slice_in_dim(p, me * quarter, quarter, 1) for p in pieces], axis=0
    )
    residual = by_neighbour(own, width).astype(F32)

    kv = dot00(w_qkv[:, width:], normed).astype(BF16)
    kv_before = shifted(kv[:, length - WINDOW :], 1)
    queries = dot00(w_qkv[:, :width], normed).astype(BF16)
    span = jnp.concatenate([kv_before, kv], axis=1)
    start = jnp.where(position == 0, WINDOW, 0).astype(jnp.int32)[None]
    heads_out = attention(start, queries, span[:width], span[width:])

    def summed(term):
        far = chip_shift(term(3))
        near = chip_shift(term(1))
        away = (term(2).astype(F32) + far.astype(F32)).astype(BF16)
        back = cross_shift(away)
        return term(0).astype(F32) + near.astype(F32) + back.astype(F32)

    def attn_term(k):
        rows = lax.dynamic_slice_in_dim(heads_out, (me ^ k) * quarter, quarter, 1)
        return dot00(w_attn_out, rows).astype(BF16)

    residual = residual + summed(attn_term)
    normed = (residual * column_scale(residual) * norm_gains[1][:, None]).astype(BF16)

    mlp_in = gathered(normed)
    w_lift = ffn[:, : 2 * hidden_width]
    w_sink = ffn[:, 2 * hidden_width :]

    def feed_forward(value):
        lifted = dot00(w_lift, value)
        hidden = (jax.nn.silu(lifted[:hidden_width]) * lifted[hidden_width:]).astype(BF16)
        return jnp.dot(w_sink, hidden, preferred_element_type=F32).astype(BF16)

    near_terms = feed_forward(jnp.concatenate(mlp_in[:2], axis=1))
    terms = [
        near_terms[:, :quarter],
        near_terms[:, quarter:],
        feed_forward(mlp_in[2]),
        feed_forward(mlp_in[3]),
    ]
    residual = residual + summed(lambda k: terms[k])
    encoded = (residual * column_scale(residual) * norm_gains[2][:, None]).astype(BF16)

    states = jnp.concatenate(gathered(encoded), axis=1)
    w_cross = jnp.concatenate([w_cross_key, w_cross_value], axis=1)
    cross_kv = dot00(w_cross, states).astype(BF16)
    left = jnp.where(chip == 0, cross_kv[:, :half], cross_kv[:, half:])
    right = jnp.where(chip == 0, cross_kv[:, half:], cross_kv[:, :half])
    from_before = shifted(right, 1)
    from_after = shifted(left, -1)
    frame = jnp.concatenate([from_before, left, right, from_after], axis=1)

    at = jnp.arange(half, dtype=jnp.int32)
    in_half = ((at // quarter) ^ core) * quarter + at % quarter
    base = position * length
    frame_pos = jnp.concatenate([base + (j - 1) * half + in_half for j in range(4)])
    state_pos = base + jnp.concatenate([chip * half + in_half, (1 - chip) * half + in_half])

    starts = jnp.concatenate([before_start, patch_start, after_start])
    ends = jnp.concatenate([starts[1:], jnp.full((1,), FAR, jnp.int32)])
    patch_count = patch_start.shape[0]
    limit = seq_count * length
    ends = jnp.minimum(ends, limit)
    covered = (state_pos[None, :] >= starts[:, None]) & (state_pos[None, :] < ends[:, None])
    sums = lax.dot_general(
        covered.astype(BF16), states, (((1,), (1,)), ((), ())), preferred_element_type=F32
    )
    sum_from_after = shifted(sums[:patch_count], -1)
    sum_from_before = shifted(sums[2 * patch_count :], 1)
    own_end = ends[patch_count : 2 * patch_count]
    counts = (own_end - patch_start).astype(F32)
    pooled = (
        sums[patch_count : 2 * patch_count] + sum_from_after + sum_from_before
    ) / counts[:, None]

    cross_queries = jnp.dot(
        pooled.astype(BF16), w_cross_query, preferred_element_type=F32
    ).astype(BF16)
    member = (frame_pos[None, :] >= patch_start[:, None]) & (frame_pos[None, :] < own_end[:, None])
    heads = width // HD
    scores = jnp.einsum(
        "phd,hdk->hpk",
        cross_queries.reshape(patch_count, heads, HD),
        frame[:width].reshape(heads, HD, 2 * length),
        preferred_element_type=F32,
    ) * HD ** (-0.5)
    scores = jnp.where(member[None], scores, -1e30)
    raised = jnp.exp(scores - jnp.max(scores, axis=-1, keepdims=True))
    weights = (raised / jnp.sum(raised, axis=-1, keepdims=True)).astype(BF16)
    cross_heads = (
        jnp.einsum(
            "hpk,hdk->phd",
            weights,
            frame[width:].reshape(heads, HD, 2 * length),
            preferred_element_type=F32,
        )
        .astype(BF16)
        .reshape(patch_count, width)
    )
    mixed = jnp.dot(cross_heads, w_cross_out, preferred_element_type=F32).astype(BF16)
    mixed_sum = mixed.astype(F32)
    for pairs in (ON_CHIP, ACROSS, DIAGONAL):
        mixed_sum = mixed_sum + lax.ppermute(mixed, "mp", pairs).astype(F32)
    patch_hidden = (pooled + mixed_sum).astype(BF16)
    return jnp.dot(patch_hidden, w_global, preferred_element_type=F32).astype(BF16)


def solution(mesh):
    return jax.shard_map(
        per_device,
        mesh=mesh,
        in_specs=(
            P("seq"),
            P("seq", None),
            P("seq"),
            P("seq"),
            P(None, "mp"),
            P("seq", "mp"),
            P(),
            P(None, "mp"),
            P(None, "mp"),
            P(None, "mp"),
            P("mp", None),
            P("seq", "mp"),
            P("seq", "mp"),
            P("mp", "seq"),
            P(None, "mp"),
            P(None, "mp"),
            P(None, "mp"),
            P("mp", None),
            P(None, "mp"),
        ),
        out_specs=P("seq", "mp"),
        check_vma=False,
    )
```

```python
import functools

import jax
import jax.numpy as jnp
from jax import lax
from jax.experimental import pallas as pl
from jax.experimental.pallas import tpu as pltpu
from jax.sharding import PartitionSpec as P

HD = 64
WINDOW = 512
REACH = 512
BLOCK = 256
PIECE = 128
SLOTS = (0, 2, 1, 3)
LAYERS = 4
FAR = 1 << 30
ON_CHIP = [(0, 1), (1, 0), (2, 3), (3, 2)]
ACROSS = [(0, 2), (2, 0), (1, 3), (3, 1)]
DIAGONAL = [(0, 3), (3, 0), (1, 2), (2, 1)]


F32 = jnp.float32
BF16 = jnp.bfloat16


def dot00(a, b):
    return lax.dot_general(a, b, (((0,), (0,)), ((), ())), preferred_element_type=F32)


def chip_shift(value):
    return lax.ppermute(value, "mp", ON_CHIP)


def cross_shift(value):
    return lax.ppermute(value, "mp", ACROSS)


def shifted(value, steps):
    count = lax.axis_size("seq")
    first, last = (max(0, -steps), min(count, count - steps))
    return lax.ppermute(value, "seq", [(i, i + steps) for i in range(first, last)])


def slot_of(neighbour):
    return (neighbour % 2) * 2 + neighbour // 2


def attend(info_ref, q_ref, kp_ref, vp_ref, k_ref, v_ref, o_ref):
    kk = lax.broadcasted_iota(jnp.int32, (BLOCK, BLOCK), 0)
    qq = lax.broadcasted_iota(jnp.int32, (BLOCK, BLOCK), 1)
    me = info_ref[0]
    live = (kk * 0 + info_ref[1]) > 0
    blocks = WINDOW // BLOCK
    for b in range(blocks):
        q = q_ref[:, b * BLOCK : (b + 1) * BLOCK]
        scores, values = [], []
        for t in range(blocks + 1):
            at = (b + t) % blocks * BLOCK
            early = b + t < blocks
            keys = (kp_ref if early else k_ref)[:, at : at + BLOCK]
            values.append((vp_ref if early else v_ref)[:, at : at + BLOCK])
            s = dot00(keys, q)
            if t == 0:
                s = jnp.where((kk > qq) & live, s, -1e30)
            elif t == blocks:
                s = jnp.where(kk <= qq, s, -1e30)
            elif early:
                s = jnp.where(live, s, -1e30)
            scores.append(s)
        highest = functools.reduce(
            jnp.maximum, [jnp.max(s, axis=0, keepdims=True) for s in scores]
        )
        total = jnp.zeros((1, BLOCK), F32)
        acc = jnp.zeros((HD, BLOCK), F32)
        for s, v in zip(scores, values):
            p = jnp.exp((s - highest) * (HD**-0.5))
            total = total + jnp.sum(p, axis=0, keepdims=True)
            acc = acc + jnp.dot(v, p.astype(BF16), preferred_element_type=F32)
        out = (acc / total).astype(BF16)
        for j in range(BLOCK // PIECE):
            neighbour = me ^ (b * (BLOCK // PIECE) + j)
            slot = (neighbour & 1) * 2 + (neighbour >> 1)
            o_ref[:, pl.ds(pl.multiple_of(slot * PIECE, PIECE), PIECE)] = out[
                :, j * PIECE : (j + 1) * PIECE
            ]


def attention(info, q, kv_before, kv):
    width, half = q.shape
    heads = width // HD
    block = functools.partial(pl.BlockSpec, (HD, half))
    return pl.pallas_call(
        attend,
        grid_spec=pltpu.PrefetchScalarGridSpec(
            num_scalar_prefetch=1,
            grid=(heads,),
            in_specs=[
                block(lambda h, s: (h, 0)),
                block(lambda h, s: (h, 0)),
                block(lambda h, s: (h + heads, 0)),
                block(lambda h, s: (h, 0)),
                block(lambda h, s: (h + heads, 0)),
            ],
            out_specs=block(lambda h, s: (h, 0)),
        ),
        out_shape=jax.ShapeDtypeStruct((width, half), BF16),
        name="attend",
    )(info, q, kv_before, kv_before, kv, kv)


def column_scale(values):
    return lax.rsqrt(jnp.mean(values * values, axis=0, keepdims=True) + 1e-05)


def together(*values):
    return lax.optimization_barrier(values)


def after(value, other):
    mark = lax.slice(other, (0,) * other.ndim, (1,) * other.ndim).reshape(())
    value, mark = lax.optimization_barrier((value, mark))
    limit = FAR if mark.dtype == jnp.int32 else 3e38
    return jnp.where(mark < jnp.asarray(limit, mark.dtype), value, jnp.zeros_like(value))


def ffn_weights(packed, layers):
    count = lax.axis_size("seq")
    plane = count // layers
    layer = lax.axis_index("seq") // plane
    column = jnp.zeros((layers, *packed.shape), packed.dtype)
    for step in range(layers):
        piece = packed
        if step:
            move = [(i, (i + step * plane) % count) for i in range(count)]
            piece = lax.ppermute(packed, "seq", move)
        column = lax.dynamic_update_slice_in_dim(
            column, piece[None], (layer - step) % layers, 0
        )
    column = column.reshape(layers * packed.shape[0], packed.shape[1])
    planes = [[z * plane + i for i in range(plane)] for z in range(layers)]
    everything = lax.all_gather(column, "seq", axis=0, axis_index_groups=planes)
    return everything.reshape(count * packed.shape[0], packed.shape[1])


def gathered_order(features, seq_count, layers):
    rows = features // seq_count
    plane = seq_count // layers
    f = jnp.arange(features, dtype=jnp.int32)
    at = (f // rows % plane) * (layers * rows) + (f // (rows * plane)) * rows + f % rows
    return (f[:, None] == at[None, :]).astype(BF16)


def per_device(
    byte_values,
    hash_owner,
    hash_slot,
    patch_start,
    byte_table,
    hash_table,
    norm_gains,
    w_query,
    w_key,
    w_value,
    w_attn_out,
    w_gate,
    w_up,
    w_down,
    w_cross_query,
    w_cross_key,
    w_cross_value,
    w_cross_out,
    w_global,
):
    seq_count = lax.axis_size("seq")
    position = lax.axis_index("seq")
    group = lax.axis_size("mp")
    me = lax.axis_index("mp")
    length = byte_values.shape[0]
    half = length // 2
    piece = half // group
    width = w_query.shape[1]
    features = w_query.shape[0]
    hidden_width = w_gate.shape[1]
    capacity = 2 * length // seq_count

    owner = hash_owner[:, 0]
    owner_hot = (owner[:, None] == jnp.arange(seq_count, dtype=jnp.int32)[None, :]).astype(BF16)
    line = jnp.arange(length, dtype=jnp.int32)
    earlier = (line[:, None] > line[None, :]).astype(BF16)
    before = jnp.dot(earlier, owner_hot, preferred_element_type=F32)
    order = jnp.sum(before * owner_hot.astype(F32), axis=1).astype(jnp.int32)
    order_hot = order[:, None] == jnp.arange(capacity, dtype=jnp.int32)[None, :]
    slot_parts = jnp.concatenate(
        [
            jnp.where(order_hot, (hash_slot // 64)[:, None], 0),
            jnp.where(order_hot, (hash_slot % 64)[:, None], 0),
        ],
        axis=1,
    ).astype(BF16)
    asked = dot00(owner_hot, slot_parts)
    requests = (asked[:, :capacity] * 64 + asked[:, capacity:]).astype(jnp.int32)
    wanted = lax.all_to_all(requests, "seq", split_axis=0, concat_axis=0, tiled=True)

    packed = jnp.concatenate([w_gate, w_up, w_down.T], axis=1)
    ffn = ffn_weights(after(packed, wanted), LAYERS)

    bounds = after(patch_start, wanted)
    before_start = shifted(bounds, 1)
    after_start = shifted(bounds, -1)
    after_start = jnp.where(position == seq_count - 1, FAR, after_start)

    found = jnp.take(hash_table, wanted, axis=0, mode="clip")
    found, w_query, w_key, w_value, norm_gains = together(
        found, w_query, w_key, w_value, norm_gains
    )
    fetched = lax.all_to_all(found, "seq", split_axis=0, concat_axis=0, tiled=True)
    fetched = fetched.reshape(seq_count * capacity, width)
    place = owner * capacity + order
    lookup = jnp.arange(seq_count * capacity, dtype=jnp.int32)[:, None]
    byte_lookup = jnp.arange(256, dtype=jnp.int32)[:, None]

    def by_slot(value):
        return jnp.concatenate(
            [lax.dynamic_slice_in_dim(value, (me ^ k) * width, width, 0) for k in SLOTS], axis=0
        )

    def from_slots(value):
        return jnp.concatenate(
            [
                lax.dynamic_slice_in_dim(value, slot_of(me ^ j) * width, width, 0)
                for j in range(group)
            ],
            axis=0,
        )

    w_q = by_slot(w_query).T
    w_kv = by_slot(jnp.concatenate([w_key, w_value], axis=1)).T
    gain_first = by_slot(norm_gains[0])
    w_cross = jnp.concatenate([w_cross_key, w_cross_value], axis=1).T
    w_out = w_attn_out.T
    to_ffn = gathered_order(features, seq_count, LAYERS)
    fetched, w_q, w_kv, w_cross, w_out, gain_first, before_start, after_start, to_ffn = together(
        fetched, w_q, w_kv, w_cross, w_out, gain_first, before_start, after_start, to_ffn
    )

    def embedded(h):
        at = slice(h * half, (h + 1) * half)
        row_hot = (lookup == place[None, at]).astype(BF16)
        byte_hot = (byte_lookup == byte_values[None, at]).astype(BF16)
        return (dot00(byte_table, byte_hot) + dot00(fetched, row_hot)).astype(BF16)

    def normed_first(x):
        x = x.astype(F32)
        return (x * column_scale(x) * gain_first[:, None]).astype(BF16)

    def own_bytes(x):
        return from_slots(lax.dynamic_slice_in_dim(x, me * piece, piece, 1)).astype(F32)

    def project(w, x):
        return jnp.dot(w, x, preferred_element_type=F32).astype(BF16)

    def gathered(value, dim, meanwhile=None):
        across = cross_shift(value)
        if meanwhile is not None:
            across = after(across, meanwhile)
        pair = jnp.concatenate([value, across], axis=dim)
        return jnp.concatenate([pair, chip_shift(pair)], axis=dim)

    embed0 = embedded(0)
    wide1 = gathered(embedded(1), 0, embed0)
    wide0 = gathered(embed0, 0)
    normed1 = normed_first(wide1)
    kv1 = project(w_kv, normed1)
    kv_before = shifted(kv1, 1)
    q1 = project(w_q, normed1)
    normed0 = normed_first(after(wide0, q1))
    kv0 = project(w_kv, normed0)
    q0 = project(w_q, normed0)
    always = jnp.ones((), jnp.int32)
    later = (position > 0).astype(jnp.int32)

    def spread(weights, value):
        return project(weights, value[:, half // 2 :])

    def joined(weights, value, beside):
        return project_wide(weights, value[:, : half // 2]) + beside.astype(F32)

    def project_wide(w, x):
        return jnp.dot(w, x, preferred_element_type=F32)

    def normed_by(x, row):
        return (x * column_scale(x) * norm_gains[row][:, None]).astype(BF16)

    def across_of(here):
        return cross_shift(here[:, piece:].astype(BF16))

    heads1 = attention(jnp.stack([me, always]), q1, kv0, kv1)
    away1 = spread(w_out, heads1)
    beside1 = chip_shift(away1)
    here1 = joined(w_out, heads1, beside1)
    back1 = across_of(here1)
    heads0 = attention(after(jnp.stack([me, later]), here1), q0, kv_before, kv0)
    residual1 = own_bytes(wide1)
    residual0 = own_bytes(wide0)
    beside0 = chip_shift(spread(w_out, heads0))
    here0 = joined(w_out, heads0, beside0)
    back0 = across_of(here0)
    back1, residual0, residual1 = together(back1, residual0, residual1)

    residual1 = residual1 + here1[:, :piece] + back1.astype(F32)
    normed1 = project(to_ffn, normed_by(residual1, 1))
    back0 = after(back0, normed1)
    mlp1 = gathered(normed1, 1)
    residual0 = residual0 + here0[:, :piece] + back0.astype(F32)
    normed0 = project(to_ffn, normed_by(residual0, 1))
    mlp0 = gathered(normed0, 1)

    w_lift = ffn[:, : 2 * hidden_width]
    w_sink = ffn[:, 2 * hidden_width :]

    def feed_forward(value):
        lifted = dot00(w_lift, value)
        return (jax.nn.silu(lifted[:hidden_width]) * lifted[hidden_width:]).astype(BF16)

    def from_ffn(value):
        high = lax.reduce_precision(value, 8, 7)
        return dot00(to_ffn, high.astype(BF16)) + dot00(to_ffn, (value - high).astype(BF16))

    hidden1 = feed_forward(mlp1)
    away1 = spread(w_sink, hidden1)
    mlp0 = after(mlp0, away1)
    beside1 = chip_shift(away1)
    here1 = joined(w_sink, hidden1, beside1)
    back1 = across_of(here1)
    hidden0 = feed_forward(mlp0)
    beside0 = chip_shift(spread(w_sink, hidden0))
    here0 = joined(w_sink, hidden0, beside0)
    back0 = across_of(here0)
    residual1 = residual1 + from_ffn(here1[:, :piece]) + dot00(to_ffn, back1)
    encoded1 = normed_by(residual1, 2)
    back0 = after(back0, encoded1)
    states1 = gathered(encoded1, 1)
    residual0 = residual0 + from_ffn(here0[:, :piece]) + dot00(to_ffn, back0)
    states0 = gathered(normed_by(residual0, 2), 1)

    cross1 = project(w_cross, states1)
    from_before = shifted(cross1, 1)
    states0 = after(states0, cross1)
    cross0 = project(w_cross, states0)
    from_after = shifted(cross0, -1)
    states = (states0, states1)
    frame = jnp.concatenate([from_before, cross0, cross1, from_after], axis=1)

    at = jnp.arange(piece, dtype=jnp.int32)
    in_half = jnp.concatenate([(me ^ k) * piece + at for k in SLOTS])
    base = position * length
    frame_pos = jnp.concatenate([base + (j - 1) * half + in_half for j in range(4)])
    state_pos = frame_pos[half : half + length]

    starts = jnp.concatenate([before_start, patch_start, after_start])
    ends = jnp.concatenate([starts[1:], jnp.full((1,), FAR, jnp.int32)])
    ends = jnp.minimum(ends, seq_count * length)
    patch_count = patch_start.shape[0]

    def sums_over(h):
        pos = state_pos[None, h * half : (h + 1) * half]
        covered = (pos >= starts[:, None]) & (pos < ends[:, None])
        return lax.dot_general(
            covered.astype(BF16), states[h], (((1,), (1,)), ((), ())), preferred_element_type=F32
        )

    sums = sums_over(1) + sums_over(0)
    sum_from_after = shifted(sums[:patch_count], -1)
    sum_from_before = shifted(sums[2 * patch_count :], 1)
    own_end = ends[patch_count : 2 * patch_count]
    counts = (own_end - patch_start).astype(F32)
    pooled = (
        sums[patch_count : 2 * patch_count] + sum_from_after + sum_from_before
    ) / counts[:, None]

    cross_queries = jnp.dot(
        pooled.astype(BF16), w_cross_query, preferred_element_type=F32
    ).astype(BF16)
    member = (frame_pos[None, :] >= patch_start[:, None]) & (frame_pos[None, :] < own_end[:, None])
    heads = width // HD
    scores = jnp.einsum(
        "phd,hdk->hpk",
        cross_queries.reshape(patch_count, heads, HD),
        frame[:width].reshape(heads, HD, 2 * length),
        preferred_element_type=F32,
    ) * HD ** (-0.5)
    scores = jnp.where(member[None], scores, -1e30)
    raised = jnp.exp(scores - jnp.max(scores, axis=-1, keepdims=True))
    weights = (raised / jnp.sum(raised, axis=-1, keepdims=True)).astype(BF16)
    cross_heads = (
        jnp.einsum(
            "hpk,hdk->phd",
            weights,
            frame[width:].reshape(heads, HD, 2 * length),
            preferred_element_type=F32,
        )
        .astype(BF16)
        .reshape(patch_count, width)
    )
    mixed = jnp.dot(cross_heads, w_cross_out, preferred_element_type=F32).astype(BF16)
    mixed_sum = mixed.astype(F32)
    for pairs in (ON_CHIP, ACROSS, DIAGONAL):
        mixed_sum = mixed_sum + lax.ppermute(mixed, "mp", pairs).astype(F32)
    patch_hidden = (pooled + mixed_sum).astype(BF16)
    return jnp.dot(patch_hidden, w_global, preferred_element_type=F32).astype(BF16)


def solution(mesh):
    return jax.shard_map(
        per_device,
        mesh=mesh,
        in_specs=(
            P("seq"),
            P("seq", None),
            P("seq"),
            P("seq"),
            P(None, "mp"),
            P("seq", "mp"),
            P(),
            P(None, "mp"),
            P(None, "mp"),
            P(None, "mp"),
            P("mp", None),
            P("seq", "mp"),
            P("seq", "mp"),
            P("mp", "seq"),
            P(None, "mp"),
            P(None, "mp"),
            P(None, "mp"),
            P("mp", None),
            P(None, "mp"),
        ),
        out_specs=P("seq", "mp"),
        check_vma=False,
    )
```
